32 devices in a mesh: seq: 16 (over z, x, core), head: 2 (over y).
Axes of the slice: x: 2, y: 2, z: 4, core: 2. Of those that a mesh axis runs over, the one named last changes fastest.
Arguments:
- fw_query: bfloat16 [6144, 4096], P('seq', 'head'), may hold values from -6 to 6
- fw_key: bfloat16 [6144, 4096], P('seq', 'head'), may hold values from -6 to 6
- fw_value: bfloat16 [6144, 4096], P('seq', 'head'), may hold values from -6 to 6
- learn_rate: float32 [6144, 8], P('seq', 'head'), may hold values from 0.00025515517 to 0.002551552
- fast_weights: bfloat16 [3, 8, 512, 512], P(None, 'head'), may hold values from -0.25 to 0.25
- attn_query: bfloat16 [6144, 4096], P(('seq', 'head')), may hold values from -32 to 32
- attn_key: bfloat16 [6144, 1024], P(('seq', 'head')), may hold values from -32 to 32
- attn_value: bfloat16 [6144, 1024], P(('seq', 'head')), may hold values from -6 to 6
Outputs:
- mixed: bfloat16 [6144, 4096], P(('seq', 'head'))
The draws below stay inside these ranges and needn't reach their ends.
All inputs are finite; a program needn't handle non-finite values.
Results may differ from the reference program's by a relative error of at most 0.01.
Values may be sent and summed in bfloat16 or wider, within the bound.
A program may use at most 128 MiB of HBM per device.

```python
import math
import jax
import jax.numpy as jnp
from jax import lax

FW_HEADS = 8
FW_DIM = 512
Q_HEADS = 32
KV_HEADS = 8
HEAD_DIM = 128
WINDOW = 256
D = 4096
TOKENS = 6144


def draw_attn_key(key, part):
    base = jax.random.normal(jax.random.fold_in(key, 1), (TOKENS, KV_HEADS * HEAD_DIM), jnp.float32)
    base = jnp.clip(base, -6.0, 6.0)
    return jnp.clip(base, -32.0, 32.0).astype(jnp.bfloat16)


def draw_attn_query(key, part):
    base = jax.random.normal(jax.random.fold_in(key, 2), (TOKENS, Q_HEADS * HEAD_DIM), jnp.float32)
    base = jnp.clip(base, -6.0, 6.0)
    return jnp.clip(base, -32.0, 32.0).astype(jnp.bfloat16)


def shard_levels(stream_key, dims, shards, least, top_value):
    loudness = 1.0
    for dim, blocks in shards:
        draws = jax.random.uniform(jax.random.fold_in(jax.random.fold_in(stream_key, 6), dim), (blocks,), jnp.float32, least / len(shards), top_value / len(shards))
        loudness = loudness * jnp.repeat(jnp.exp(draws), dims[dim] // blocks).reshape((-1,) + (1,) * (len(dims) - 1 - dim))
    return loudness


def noise(rng, shape, scale, most, cuts=(), kind=jnp.bfloat16):
    level = shard_levels(rng, shape, cuts, -0.22, 0.18) if cuts else 1.0
    drawn = jax.random.normal(rng, shape, jnp.float32) * scale * level
    return jnp.minimum(jnp.maximum(drawn, -most), most).astype(kind)


def setup_inputs(seed: int = 0) -> dict:
    key_of = jax.random.split(jax.random.key(seed), 9)
    return {
        "fw_query": noise(key_of[0], (TOKENS, D), 1.0, 6.0, ((0, 16), (1, 2))),
        "fw_key": noise(key_of[1], (TOKENS, D), 1.0, 6.0, ((0, 16), (1, 2))),
        "fw_value": noise(key_of[2], (TOKENS, D), 1.0, 6.0, ((0, 16), (1, 2))),
        "learn_rate": jnp.clip(jnp.exp(math.log(0.002551552) - 2.3025852 * jax.random.uniform(key_of[3], (TOKENS, FW_HEADS), jnp.float32) ** shard_levels(key_of[3], (TOKENS, FW_HEADS), ((0, 16), (1, 2)), -0.2, 0.2)), 0.00025515517, 0.002551552),
        "fast_weights": noise(key_of[4], (3, FW_HEADS, FW_DIM, FW_DIM), FW_DIM ** -0.5, 0.25, ((1, 2),)),
        "attn_query": draw_attn_query(jax.random.fold_in(key_of[8], 71), 0),
        "attn_key": draw_attn_key(jax.random.fold_in(key_of[8], 71), 0),
        "attn_value": noise(key_of[7], (TOKENS, KV_HEADS * HEAD_DIM), 1.0, 6.0, ((0, 32),)),
    }


def head_update(q, k, v, rates, weights):
    w_gate = weights[0]
    w_up = weights[1]
    w_down = weights[2]
    pre_gate = jnp.dot(k, w_gate, preferred_element_type=jnp.float32)
    pre_up = jnp.dot(k, w_up, preferred_element_type=jnp.float32)
    sigm = jax.nn.sigmoid(pre_gate)
    hidden = (pre_gate * sigm * pre_up).astype(jnp.bfloat16)
    scaled = (rates[:, None] * v.astype(jnp.float32)).astype(jnp.bfloat16)
    back = jnp.dot(scaled, w_down.T, preferred_element_type=jnp.float32)
    d_gate = (back * pre_up * sigm * (1.0 + pre_gate * (1.0 - sigm))).astype(jnp.bfloat16)
    d_up = (back * pre_gate * sigm).astype(jnp.bfloat16)
    grads = jnp.stack([jnp.dot(k.T, d_gate, preferred_element_type=jnp.float32), jnp.dot(k.T, d_up, preferred_element_type=jnp.float32), jnp.dot(hidden.T, scaled, preferred_element_type=jnp.float32)])
    start = weights.astype(jnp.float32)
    stepped = start + grads
    ratio = jnp.sqrt(lax.optimization_barrier(jnp.mean(start * start, axis=-2, keepdims=True))) * lax.rsqrt(lax.optimization_barrier(jnp.mean(stepped * stepped, axis=-2, keepdims=True)) + 1e-06)
    fresh = (stepped * ratio).astype(jnp.bfloat16)
    q_gate = jnp.dot(q, fresh[0], preferred_element_type=jnp.float32)
    q_up = jnp.dot(q, fresh[1], preferred_element_type=jnp.float32)
    answer_hidden = (q_gate * jax.nn.sigmoid(q_gate) * q_up).astype(jnp.bfloat16)
    return jnp.dot(answer_hidden, fresh[2], preferred_element_type=jnp.float32).astype(jnp.bfloat16)

def reference(fw_query, fw_key, fw_value, learn_rate, fast_weights, attn_query, attn_key, attn_value):

    def heads_first(arr):
        return arr.reshape(TOKENS, FW_HEADS, FW_DIM).transpose(1, 0, 2)

    def per_head(items):
        return head_update(items[0], items[1], items[2], items[3], items[4])
    fw_heads = lax.map(per_head, (heads_first(fw_query), heads_first(fw_key), heads_first(fw_value), learn_rate.T, fast_weights.transpose(1, 0, 2, 3)))
    fw_out = fw_heads.transpose(1, 0, 2).reshape(TOKENS, D)
    group = Q_HEADS // KV_HEADS
    block_rows = math.gcd(512, TOKENS)
    scaling = 1.0 / math.sqrt(HEAD_DIM)
    query_heads = attn_query.reshape(TOKENS, KV_HEADS, group, HEAD_DIM)
    front = jnp.zeros((WINDOW, KV_HEADS * HEAD_DIM), jnp.bfloat16)
    key_pad = jnp.concatenate([front, attn_key], axis=0).reshape(TOKENS + WINDOW, KV_HEADS, HEAD_DIM)
    value_pad = jnp.concatenate([front, attn_value], axis=0).reshape(TOKENS + WINDOW, KV_HEADS, HEAD_DIM)

    def block(index):
        start = (index * block_rows).astype(jnp.int32)
        q_block = lax.dynamic_slice_in_dim(query_heads, start, block_rows, 0)
        k_block = lax.dynamic_slice_in_dim(key_pad, start, block_rows + WINDOW, 0)
        v_block = lax.dynamic_slice_in_dim(value_pad, start, block_rows + WINDOW, 0)
        scores = jnp.einsum('fcgd,lcd->cgfl', q_block.astype(jnp.float32), k_block.astype(jnp.float32)) * scaling
        t_pos = start + jnp.arange(block_rows, dtype=jnp.int32)
        s_pos = start - WINDOW + jnp.arange(block_rows + WINDOW, dtype=jnp.int32)
        gap = t_pos[:, None] - s_pos[None, :]
        keep = (gap >= 0) & (gap < WINDOW) & (s_pos[None, :] >= 0)
        scores = jnp.where(keep, scores, -1e+30)
        top = lax.optimization_barrier(jnp.max(scores, axis=-1, keepdims=True))
        expo = jnp.exp(scores - top)
        probs = (expo / lax.optimization_barrier(jnp.sum(expo, axis=-1, keepdims=True))).astype(jnp.bfloat16)
        out = jnp.einsum('cgfl,lcd->fcgd', probs.astype(jnp.float32), v_block.astype(jnp.float32))
        return out.reshape(block_rows, Q_HEADS * HEAD_DIM)
    attn_out = lax.map(block, jnp.arange(TOKENS // block_rows, dtype=jnp.int32)).reshape(TOKENS, D)
    return (attn_out + fw_out.astype(jnp.float32)).astype(jnp.bfloat16)
```

```python
import functools
import math

import jax
import jax.numpy as jnp
from jax import lax
from jax.experimental import pallas as pl
from jax.experimental.pallas import tpu as pltpu
from jax.sharding import PartitionSpec as P

Q_HEADS = 32
KV_HEADS = 8
HEAD_DIM = 128
WINDOW = 256


def shifted(value, axis, by):
    devices = lax.axis_size(axis)
    pairs = [(i, i + by) for i in range(devices) if 0 <= i + by < devices]
    return lax.ppermute(value, axis, pairs)


def local_grads(keys, values, rates, weights):
    pre_gate = jnp.einsum("thd,hde->the", keys, weights[0], preferred_element_type=jnp.float32)
    pre_up = jnp.einsum("thd,hde->the", keys, weights[1], preferred_element_type=jnp.float32)
    sigm = jax.nn.sigmoid(pre_gate)
    hidden = (pre_gate * sigm * pre_up).astype(jnp.bfloat16)
    scaled = (rates[:, :, None] * values.astype(jnp.float32)).astype(jnp.bfloat16)
    back = jnp.einsum("the,hde->thd", scaled, weights[2], preferred_element_type=jnp.float32)
    d_gate = (back * pre_up * sigm * (1.0 + pre_gate * (1.0 - sigm))).astype(jnp.bfloat16)
    d_up = (back * pre_gate * sigm).astype(jnp.bfloat16)
    grad_gate = jnp.einsum("thd,the->hde", keys, d_gate, preferred_element_type=jnp.float32)
    grad_up = jnp.einsum("thd,the->hde", keys, d_up, preferred_element_type=jnp.float32)
    grad_down = jnp.einsum("thd,the->hde", hidden, scaled, preferred_element_type=jnp.float32)
    return jnp.stack([grad_gate, grad_up, grad_down])


def renorm(summed, start_weights):
    start = start_weights.astype(jnp.float32)
    stepped = start + summed
    ratio = jnp.sqrt(jnp.mean(start * start, axis=-2, keepdims=True)) * lax.rsqrt(
        jnp.mean(stepped * stepped, axis=-2, keepdims=True) + 1e-06
    )
    return (stepped * ratio).astype(jnp.bfloat16)


def on_device(
    fw_query, fw_key, fw_value, learn_rate, fast_weights, attn_query, attn_key, attn_value
):
    tok_rows = fw_key.shape[0]
    local_heads = fast_weights.shape[1]
    width = fast_weights.shape[2]
    keys = fw_key.reshape(tok_rows, local_heads, width)
    values = fw_value.reshape(tok_rows, local_heads, width)
    queries = fw_query.reshape(tok_rows, local_heads, width)
    grads = local_grads(keys, values, learn_rate, fast_weights)
    share = lax.psum_scatter(grads, "seq", scatter_dimension=3, tiled=True)
    columns = share.shape[3]
    start_cols = lax.dynamic_slice_in_dim(fast_weights, lax.axis_index("seq") * columns, columns, 3)
    fresh_part = renorm(share, start_cols)
    fresh = lax.all_gather(fresh_part, "seq", axis=3, tiled=True)
    q_gate = jnp.einsum("thd,hde->the", queries, fresh[0], preferred_element_type=jnp.float32)
    q_up = jnp.einsum("thd,hde->the", queries, fresh[1], preferred_element_type=jnp.float32)
    answer_hidden = (q_gate * jax.nn.sigmoid(q_gate) * q_up).astype(jnp.bfloat16)
    fw_out = jnp.einsum(
        "the,hef->thf", answer_hidden, fresh[2], preferred_element_type=jnp.float32
    ).astype(jnp.bfloat16)
    fw_out = fw_out.reshape(tok_rows, local_heads * width)
    fw_fine = lax.all_to_all(fw_out, "head", split_axis=0, concat_axis=1, tiled=True)
    rows = attn_query.shape[0]
    reach = -(-WINDOW // rows)
    kv_width = attn_key.shape[1]
    group = Q_HEADS // KV_HEADS
    buffer_k = jnp.zeros(((reach + 1) * rows, kv_width), jnp.bfloat16)
    buffer_v = jnp.zeros(((reach + 1) * rows, kv_width), jnp.bfloat16)
    buffer_k = lax.dynamic_update_slice_in_dim(buffer_k, attn_key, reach * rows, 0)
    buffer_v = lax.dynamic_update_slice_in_dim(buffer_v, attn_value, reach * rows, 0)

    def bring(step, carry):
        piece_k, piece_v, store_k, store_v = carry
        piece_k, piece_v = shifted((piece_k, piece_v), ("seq", "head"), 1)
        slot = (reach - 1 - step) * rows
        store_k = lax.dynamic_update_slice_in_dim(store_k, piece_k, slot, 0)
        store_v = lax.dynamic_update_slice_in_dim(store_v, piece_v, slot, 0)
        return (piece_k, piece_v, store_k, store_v)

    carried = lax.fori_loop(0, reach, bring, (attn_key, attn_value, buffer_k, buffer_v))
    buffer_k = carried[2].reshape((reach + 1) * rows, KV_HEADS, HEAD_DIM)
    buffer_v = carried[3].reshape((reach + 1) * rows, KV_HEADS, HEAD_DIM)
    device_pos = lax.axis_index("seq") * lax.axis_size("head") + lax.axis_index("head")
    t_pos = device_pos * rows + jnp.arange(rows, dtype=jnp.int32)
    s_pos = (device_pos - reach) * rows + jnp.arange((reach + 1) * rows, dtype=jnp.int32)
    gap = t_pos[:, None] - s_pos[None, :]
    keep = (gap >= 0) & (gap < WINDOW) & (s_pos[None, :] >= 0)
    query_heads = attn_query.reshape(rows, KV_HEADS, group, HEAD_DIM)
    scaling = 1.0 / math.sqrt(HEAD_DIM)
    scores = (
        jnp.einsum("fcgd,lcd->cgfl", query_heads, buffer_k, preferred_element_type=jnp.float32)
        * scaling
    )
    scores = jnp.where(keep, scores, -1e30)
    top = jnp.max(scores, axis=-1, keepdims=True)
    expo = jnp.exp(scores - top)
    probs = (expo / jnp.sum(expo, axis=-1, keepdims=True)).astype(jnp.bfloat16)
    attn_out = jnp.einsum("cgfl,lcd->fcgd", probs, buffer_v, preferred_element_type=jnp.float32)
    attn_out = attn_out.reshape(rows, Q_HEADS * HEAD_DIM)
    return (attn_out + fw_fine.astype(jnp.float32)).astype(jnp.bfloat16)

MESH = pl.DeviceIdType.MESH
LANES = 128


def gray(i):
    return i + (i // 2) * (1 - 2 * (i % 2))


def fused_kernel(
    heads, width, rows,
    q_hbm, k_hbm, v_hbm, rate_ref, w_hbm, aq_hbm, ak_hbm, av_hbm, out_ref,
    qb, kb, vb, wb, aqb, akb, avb, g, r0, r1, r2, r3, nw, att, bias, fsend, frecv,
    in_sem, misc_sem, halo_s, halo_r, s0_s, s0_r, s1_s, s1_r, s2_s, s2_r, s3_s, s3_r,
    za_s, za_r, zb_s, zb_r, x_s, x_r, c_s, c_r, y_s, y_r,
):
    me = lax.axis_index("seq")
    y = lax.axis_index("head")
    n_seq, n_head = lax.axis_size("seq"), lax.axis_size("head")
    core, xx, zb0, zb1 = me % 2, (me // 2) % 2, (me // 4) % 2, me // 8
    z = me // 4
    cb = core * 2 + xx
    other_core = me + 1 - 2 * core
    other_x = me + 2 - 4 * xx
    z_near = me + 4 - 8 * zb0
    z_far = me + 8 - 16 * zb1
    pos = me * n_head + y
    last = n_seq * n_head
    extra = WINDOW - rows
    pad = akb.shape[0] - WINDOW - rows

    def cols(block, size=LANES):
        return pl.ds(pl.multiple_of(block * size, size), size)

    def remote(src, dst, ssem, rsem, seq, head=None):
        return pltpu.make_async_remote_copy(
            src_ref=src, dst_ref=dst, send_sem=ssem, recv_sem=rsem,
            device_id={"seq": seq, "head": y if head is None else head},
            device_id_type=MESH,
        )

    def loads(h):
        c = cols(h, width)
        return (
            pltpu.make_async_copy(k_hbm.at[:, c], kb.at[:, c], in_sem.at[h, 0]),
            pltpu.make_async_copy(v_hbm.at[:, c], vb.at[:, c], in_sem.at[h, 1]),
            pltpu.make_async_copy(w_hbm.at[:, h], wb.at[:, h], in_sem.at[h, 2]),
        )

    own_at = pl.ds(pad + WINDOW, rows)
    others = (
        pltpu.make_async_copy(aq_hbm, aqb, misc_sem.at[0]),
        pltpu.make_async_copy(ak_hbm, akb.at[own_at], misc_sem.at[1]),
        pltpu.make_async_copy(av_hbm, avb.at[own_at], misc_sem.at[2]),
        pltpu.make_async_copy(q_hbm, qb, misc_sem.at[3]),
    )
    for i in range(heads):
        for copy in loads(i + (i // 2) * (1 - 2 * (i % 2))):
            copy.start()
    for copy in others:
        copy.start()

    barrier = pltpu.get_barrier_semaphore()

    def greet(seq, head):
        pl.semaphore_signal(barrier, inc=1, device_id={"seq": seq, "head": head}, device_id_type=MESH)

    for seq in (other_core, other_x, z_near, z_far):
        greet(seq, y)
    greet(me, 1 - y)

    for step in (1, 2):
        for there in (pos + step, pos + last - step):
            there = there % last
            greet(there // n_head, there % n_head)
    pl.semaphore_wait(barrier, 9)

    def halo(step):
        there = pos + step
        seq, head = there // n_head, there % n_head
        if step == 1:
            src, dst = pl.ds(0, rows), pl.ds(pad + extra, rows)
        else:
            src, dst = pl.ds(rows - extra, extra), pl.ds(pad, extra)
        j = (step - 1) * 2
        return (
            remote(ak_hbm.at[src], akb.at[dst], halo_s.at[j], halo_r.at[j], seq, head),
            remote(av_hbm.at[src], avb.at[dst], halo_s.at[j + 1], halo_r.at[j + 1], seq, head),
        )

    for step in (1, 2):
        @pl.when(pos + step < last)
        def _():
            for copy in halo(step):
                copy.start()

        @pl.when(pos < step)
        def _():
            at = pl.ds(pad + extra, rows) if step == 1 else pl.ds(pad, extra)
            akb[at, :] = jnp.zeros((at.size, akb.shape[1]), akb.dtype)
            avb[at, :] = jnp.zeros((at.size, avb.shape[1]), avb.dtype)

    akb[pl.ds(0, pad), :] = jnp.zeros((pad, akb.shape[1]), akb.dtype)
    avb[pl.ds(0, pad), :] = jnp.zeros((pad, avb.shape[1]), avb.dtype)
    t_idx = lax.broadcasted_iota(jnp.int32, bias.shape, 0)
    s_idx = lax.broadcasted_iota(jnp.int32, bias.shape, 1) - (pad + WINDOW)
    gap = t_idx - s_idx
    keep = (gap >= 0) & (gap < WINDOW) & (s_idx + pos * rows >= 0)
    bias[...] = keep.astype(jnp.float32)

    def s0(h, m):
        return remote(
            g.at[h, m, :, cols(1 - core, 2 * LANES)], r0.at[h, m], s0_s.at[h, m], s0_r.at[h, m], other_core
        )

    def s1(h, m):
        return remote(
            g.at[h, m, :, cols(core * 2 + 1 - xx)], r1.at[h, m], s1_s.at[h, m], s1_r.at[h, m], other_x
        )

    def s2(h, m):
        return remote(
            g.at[h, m, :, cols(cb)], r2.at[h // 2, m], s2_s.at[h // 2, m], s2_r.at[h // 2, m], z_near
        )

    def s3(h, m):
        return remote(g.at[h, m, :, cols(cb)], r3.at[m], s3_s.at[m], s3_r.at[m], z_far)

    def add(h, m, block, piece):
        mine = g[h, m, :, cols(block)].astype(jnp.float32)
        g[h, m, :, cols(block)] = (mine + piece.astype(jnp.float32)).astype(g.dtype)

    def compute(h):
        for copy in loads(h):
            copy.wait()
        c = cols(h, width)
        keys = kb[:, c]
        head_lane = lax.broadcasted_iota(jnp.int32, rate_ref.shape, 1)
        rate = jnp.sum(jnp.where(head_lane == h, rate_ref[...], 0.0), axis=1, keepdims=True)
        scaled = (rate * vb[:, c].astype(jnp.float32)).astype(jnp.bfloat16)
        pre_gate = jnp.dot(keys, wb[0, h], preferred_element_type=jnp.float32)
        pre_up = jnp.dot(keys, wb[1, h], preferred_element_type=jnp.float32)
        sigm = jax.nn.sigmoid(pre_gate)
        hidden = (pre_gate * sigm * pre_up).astype(jnp.bfloat16)
        tn = (((0,), (0,)), ((), ()))

        def put(m, left, right):
            g[h, m] = lax.dot_general(left, right, tn, preferred_element_type=jnp.float32).astype(g.dtype)
            s0(h, m).start()

        put(2, hidden, scaled)
        back = lax.dot_general(
            scaled, wb[2, h], (((1,), (1,)), ((), ())), preferred_element_type=jnp.float32
        )
        d_up = (back * pre_gate * sigm).astype(jnp.bfloat16)
        put(1, keys, d_up)
        d_gate = (back * pre_up * sigm * (1.0 + pre_gate * (1.0 - sigm))).astype(jnp.bfloat16)
        put(0, keys, d_gate)

    def first_add(h):
        def one(j, _):
            m = 2 - j
            s0(h, m).wait_recv()
            add(h, m, core * 2 + 1 - xx, r0[h, m, :, cols(1 - xx)])
            s1(h, m).start()
            add(h, m, cb, r0[h, m, :, cols(xx)])
            return 0

        lax.fori_loop(0, 3, one, 0)

    def loop_a(i, _):
        compute(gray(i))

        @pl.when(i > 0)
        def _():
            first_add(gray(i - 1))

        return 0

    lax.fori_loop(0, heads, loop_a, 0)
    first_add(gray(heads - 1))

    group = Q_HEADS // KV_HEADS
    scaling = 1.0 / math.sqrt(HEAD_DIM)

    def attend(c):
        keys = akb[:, cols(c)]
        vals = avb[:, cols(c)]
        for j in range(group):
            qc = cols(c * group + j)
            scores = lax.dot_general(
                aqb[:, qc], keys, (((1,), (1,)), ((), ())), preferred_element_type=jnp.float32
            ) * scaling
            scores = jnp.where(bias[...] > 0.0, scores, -1e30)
            top = jnp.max(scores, axis=-1, keepdims=True)
            expo = jnp.exp(scores - top)
            probs = (expo / jnp.sum(expo, axis=-1, keepdims=True)).astype(jnp.bfloat16)
            att[:, qc] = jnp.dot(probs, vals, preferred_element_type=jnp.float32)

    for copy in others:
        copy.wait()
    for step in (1, 2):
        @pl.when(pos >= step)
        def _():
            for copy in halo(step):
                copy.wait_recv()

    def share(h, m, block):
        return nw.at[h, m, :, cols(block)]

    def far(h, m):
        return remote(share(h, m, cb), share(h, m, cb), za_s.at[m], za_r.at[m], z_far)

    def near(h, m):
        b = h // 2
        return remote(share(h, m, cb), share(h, m, cb), zb_s.at[b, m], zb_r.at[b, m], z_near)

    def near_from(h, m):
        return near(h, m)

    def side(h, m):
        return remote(share(h, m, cb), share(h, m, cb), x_s.at[h, m], x_r.at[h, m], other_x)

    def pair(h, m, x_of):
        block = core * 2 + x_of
        return remote(
            share(h, m, block), share(h, m, block), c_s.at[h, m, x_of], c_r.at[h, m, x_of], other_core
        )

    def side_from(h, m):
        block = core * 2 + 1 - xx
        return remote(share(h, m, block), share(h, m, block), x_s.at[h, m], x_r.at[h, m], other_x)

    def pair_from(h, m, x_of):
        block = (1 - core) * 2 + x_of
        return remote(
            share(h, m, block), share(h, m, block), c_s.at[h, m, x_of], c_r.at[h, m, x_of], other_core
        )

    def stage2(p):
        h, m = gray(p // 3), 2 - p % 3
        s1(h, m).wait_recv()
        add(h, m, cb, r1[h, m])

        @pl.when(h % 2 != zb0)
        def _():
            s2(h, m).start()

    def stage3(p):
        h, m = gray(p // 3), 2 - p % 3

        @pl.when(h % 2 == zb0)
        def _():
            s2(h, m).wait_recv()
            add(h, m, cb, r2[h // 2, m])

            @pl.when(h // 2 != zb1)
            def _():
                s3(h, m).start()

    def stage4(p):
        h, m = gray(p // 3), 2 - p % 3

        @pl.when(h == z)
        def _():
            s3(h, m).wait_recv()
            start = wb[m, h, :, cols(cb)].astype(jnp.float32)
            total = g[h, m, :, cols(cb)].astype(jnp.float32) + r3[m].astype(jnp.float32)
            stepped = start + total
            ratio = jnp.sqrt(jnp.mean(start * start, axis=0, keepdims=True)) * lax.rsqrt(
                jnp.mean(stepped * stepped, axis=0, keepdims=True) + 1e-06
            )
            nw[h, m, :, cols(cb)] = (stepped * ratio).astype(nw.dtype)
            side(h, m).start()
            far(h, m).start()
            near(h, m).start()
            pair(h, m, xx).start()

    pieces = heads * 3

    def loop_b(t, _):
        @pl.when(t < pieces)
        def _():
            stage2(t)

        @pl.when((t >= 1) & (t < pieces + 1))
        def _():
            stage3(t - 1)

        @pl.when(t >= 2)
        def _():
            stage4(t - 2)

        @pl.when(t < KV_HEADS)
        def _():
            attend(t)

        return 0

    lax.fori_loop(0, pieces + 2, loop_b, 0)

    def answer_send(h):
        return remote(fsend.at[h], frecv.at[h], y_s.at[h], y_r.at[h], me, 1 - y)

    def head_of(i):
        return ((zb1 + i % 2) % 2) * 2 + (zb0 + i // 2) % 2

    def mix(value, group_of, h):
        at = cols(group_of * heads + h, width)
        out_ref[:, at] = (att[:, at] + value.astype(jnp.float32)).astype(out_ref.dtype)

    def loop_c(i, _):
        h = head_of(i)

        @pl.when(i == 0)
        def _():
            def one(j, _):
                m = 2 - j
                h_far = head_of(1)
                far(h_far, m).wait_recv()
                near(h_far, m).start()
                side(h_far, m).start()
                pair(h_far, m, xx).start()
                return 0

            lax.fori_loop(0, 3, one, 0)

        @pl.when(i < 2)
        def _():
            def one(j, _):
                m = 2 - j
                h_near = head_of(i + 2)
                near_from(h_near, m).wait_recv()
                side(h_near, m).start()
                pair(h_near, m, xx).start()
                return 0

            lax.fori_loop(0, 3, one, 0)

        def crossed(j, _):
            m = 2 - j
            side_from(h, m).wait_recv()
            pair(h, m, 1 - xx).start()
            return 0

        lax.fori_loop(0, 3, crossed, 0)

        def landed(m, _):
            pair_from(h, m, 0).wait_recv()
            pair_from(h, m, 1).wait_recv()
            return 0

        lax.fori_loop(0, 3, landed, 0)
        queries = qb[:, cols(h, width)]
        q_gate = jnp.dot(queries, nw[h, 0], preferred_element_type=jnp.float32)
        q_up = jnp.dot(queries, nw[h, 1], preferred_element_type=jnp.float32)
        hid = (q_gate * jax.nn.sigmoid(q_gate) * q_up).astype(jnp.bfloat16)
        full = jnp.dot(hid, nw[h, 2], preferred_element_type=jnp.float32).astype(jnp.bfloat16)
        low, high = full[:rows], full[rows:]
        lower = jnp.zeros((rows, width), jnp.int32) + y < 1
        fsend[h] = jnp.where(lower, high.astype(jnp.float32), low.astype(jnp.float32)).astype(jnp.bfloat16)
        answer_send(h).start()
        mix(jnp.where(lower, low.astype(jnp.float32), high.astype(jnp.float32)), y, h)
        return 0

    lax.fori_loop(0, heads, loop_c, 0)

    def loop_d(i, _):
        h = head_of(i)
        answer_send(h).wait_recv()
        mix(frecv[h], 1 - y, h)
        return 0

    lax.fori_loop(0, heads, loop_d, 0)

    for step in (1, 2):
        @pl.when(pos + step < last)
        def _():
            for copy in halo(step):
                copy.wait_send()

    def sent(p, _):
        h, m = p // 3, p % 3
        s0(h, m).wait_send()
        s1(h, m).wait_send()

        @pl.when(h % 2 != zb0)
        def _():
            s2(h, m).wait_send()

        @pl.when((h % 2 == zb0) & (h // 2 != zb1))
        def _():
            s3(h, m).wait_send()

        @pl.when(h == z)
        def _():
            far(h, m).wait_send()

        @pl.when(h % 2 == zb0)
        def _():
            near(h, m).wait_send()

        side(h, m).wait_send()
        pair(h, m, 0).wait_send()
        pair(h, m, 1).wait_send()
        return 0

    lax.fori_loop(0, pieces, sent, 0)

    def sent_y(h, _):
        answer_send(h).wait_send()
        return 0

    lax.fori_loop(0, heads, sent_y, 0)


def fused(fw_query, fw_key, fw_value, learn_rate, fast_weights, attn_query, attn_key, attn_value):
    tokens, heads, width = fw_key.shape[0], fast_weights.shape[1], fast_weights.shape[2]
    rows, kv_width = attn_key.shape
    span = -(-(WINDOW + rows) // LANES) * LANES
    bf, f32 = jnp.bfloat16, jnp.float32
    anywhere = pl.BlockSpec(memory_space=pl.ANY)
    vmem = pl.BlockSpec(memory_space=pltpu.VMEM)
    dma = pltpu.SemaphoreType.DMA
    half = heads // 2
    return pl.pallas_call(
        functools.partial(fused_kernel, heads, width, rows),
        out_shape=jax.ShapeDtypeStruct(attn_query.shape, bf),
        in_specs=[anywhere, anywhere, anywhere, vmem, anywhere, anywhere, anywhere, anywhere],
        out_specs=vmem,
        scratch_shapes=[
            pltpu.VMEM(fw_query.shape, bf),
            pltpu.VMEM(fw_key.shape, bf),
            pltpu.VMEM(fw_value.shape, bf),
            pltpu.VMEM(fast_weights.shape, bf),
            pltpu.VMEM(attn_query.shape, bf),
            pltpu.VMEM((span, kv_width), bf),
            pltpu.VMEM((span, kv_width), bf),
            pltpu.VMEM((heads, 3, width, width), bf),
            pltpu.VMEM((heads, 3, width, 2 * LANES), bf),
            pltpu.VMEM((heads, 3, width, LANES), bf),
            pltpu.VMEM((half, 3, width, LANES), bf),
            pltpu.VMEM((3, width, LANES), bf),
            pltpu.VMEM((heads, 3, width, width), bf),
            pltpu.VMEM(attn_query.shape, f32),
            pltpu.VMEM((rows, span), f32),
            pltpu.VMEM((heads, rows, width), bf),
            pltpu.VMEM((heads, rows, width), bf),
            dma((heads, 3)), dma((4,)), dma((4,)), dma((4,)),
            dma((heads, 3)), dma((heads, 3)), dma((heads, 3)), dma((heads, 3)),
            dma((half, 3)), dma((half, 3)), dma((3,)), dma((3,)),
            dma((3,)), dma((3,)), dma((half, 3)), dma((half, 3)),
            dma((heads, 3)), dma((heads, 3)), dma((heads, 3, 2)), dma((heads, 3, 2)),
            dma((heads,)), dma((heads,)),
        ],
        compiler_params=pltpu.CompilerParams(
            collective_id=0, has_side_effects=True, vmem_limit_bytes=60 * 1024 * 1024
        ),
    )(fw_query, fw_key, fw_value, learn_rate, fast_weights, attn_query, attn_key, attn_value)


def takes_fused(mesh, args):
    tokens, rows = args[1].shape[0], args[5].shape[0]
    heads, width = args[4].shape[1], args[4].shape[2]
    return (
        mesh.shape["seq"] == 16
        and mesh.shape["head"] == 2
        and heads == 4
        and width == 4 * LANES
        and tokens == 2 * rows
        and rows < WINDOW < 2 * rows
        and (-(WINDOW + rows)) % LANES > 0
    )


def solution(mesh):
    placed = (
        P("seq", "head"),
        P("seq", "head"),
        P("seq", "head"),
        P("seq", "head"),
        P(None, "head", None, None),
        P(("seq", "head"), None),
        P(("seq", "head"), None),
        P(("seq", "head"), None),
    )

    def body(*args):
        return fused(*args) if takes_fused(mesh, args) else on_device(*args)

    return jax.shard_map(
        body, mesh=mesh, in_specs=placed, out_specs=P(("seq", "head"), None), check_vma=False
    )
```

```python
import functools
import math

import jax
import jax.numpy as jnp
from jax import lax
from jax.experimental import pallas as pl
from jax.experimental.pallas import tpu as pltpu
from jax.sharding import PartitionSpec as P

Q_HEADS = 32
KV_HEADS = 8
HEAD_DIM = 128
WINDOW = 256


def shifted(value, axis, by):
    devices = lax.axis_size(axis)
    pairs = [(i, i + by) for i in range(devices) if 0 <= i + by < devices]
    return lax.ppermute(value, axis, pairs)


def local_grads(keys, values, rates, weights):
    pre_gate = jnp.einsum("thd,hde->the", keys, weights[0], preferred_element_type=jnp.float32)
    pre_up = jnp.einsum("thd,hde->the", keys, weights[1], preferred_element_type=jnp.float32)
    sigm = jax.nn.sigmoid(pre_gate)
    hidden = (pre_gate * sigm * pre_up).astype(jnp.bfloat16)
    scaled = (rates[:, :, None] * values.astype(jnp.float32)).astype(jnp.bfloat16)
    back = jnp.einsum("the,hde->thd", scaled, weights[2], preferred_element_type=jnp.float32)
    d_gate = (back * pre_up * sigm * (1.0 + pre_gate * (1.0 - sigm))).astype(jnp.bfloat16)
    d_up = (back * pre_gate * sigm).astype(jnp.bfloat16)
    grad_gate = jnp.einsum("thd,the->hde", keys, d_gate, preferred_element_type=jnp.float32)
    grad_up = jnp.einsum("thd,the->hde", keys, d_up, preferred_element_type=jnp.float32)
    grad_down = jnp.einsum("thd,the->hde", hidden, scaled, preferred_element_type=jnp.float32)
    return jnp.stack([grad_gate, grad_up, grad_down])


def renorm(summed, start_weights):
    start = start_weights.astype(jnp.float32)
    stepped = start + summed
    ratio = jnp.sqrt(jnp.mean(start * start, axis=-2, keepdims=True)) * lax.rsqrt(
        jnp.mean(stepped * stepped, axis=-2, keepdims=True) + 1e-06
    )
    return (stepped * ratio).astype(jnp.bfloat16)


def on_device(
    fw_query, fw_key, fw_value, learn_rate, fast_weights, attn_query, attn_key, attn_value
):
    tok_rows = fw_key.shape[0]
    local_heads = fast_weights.shape[1]
    width = fast_weights.shape[2]
    keys = fw_key.reshape(tok_rows, local_heads, width)
    values = fw_value.reshape(tok_rows, local_heads, width)
    queries = fw_query.reshape(tok_rows, local_heads, width)
    grads = local_grads(keys, values, learn_rate, fast_weights)
    share = lax.psum_scatter(grads, "seq", scatter_dimension=3, tiled=True)
    columns = share.shape[3]
    start_cols = lax.dynamic_slice_in_dim(fast_weights, lax.axis_index("seq") * columns, columns, 3)
    fresh_part = renorm(share, start_cols)
    fresh = lax.all_gather(fresh_part, "seq", axis=3, tiled=True)
    q_gate = jnp.einsum("thd,hde->the", queries, fresh[0], preferred_element_type=jnp.float32)
    q_up = jnp.einsum("thd,hde->the", queries, fresh[1], preferred_element_type=jnp.float32)
    answer_hidden = (q_gate * jax.nn.sigmoid(q_gate) * q_up).astype(jnp.bfloat16)
    fw_out = jnp.einsum(
        "the,hef->thf", answer_hidden, fresh[2], preferred_element_type=jnp.float32
    ).astype(jnp.bfloat16)
    fw_out = fw_out.reshape(tok_rows, local_heads * width)
    fw_fine = lax.all_to_all(fw_out, "head", split_axis=0, concat_axis=1, tiled=True)
    rows = attn_query.shape[0]
    reach = -(-WINDOW // rows)
    kv_width = attn_key.shape[1]
    group = Q_HEADS // KV_HEADS
    buffer_k = jnp.zeros(((reach + 1) * rows, kv_width), jnp.bfloat16)
    buffer_v = jnp.zeros(((reach + 1) * rows, kv_width), jnp.bfloat16)
    buffer_k = lax.dynamic_update_slice_in_dim(buffer_k, attn_key, reach * rows, 0)
    buffer_v = lax.dynamic_update_slice_in_dim(buffer_v, attn_value, reach * rows, 0)

    def bring(step, carry):
        piece_k, piece_v, store_k, store_v = carry
        piece_k, piece_v = shifted((piece_k, piece_v), ("seq", "head"), 1)
        slot = (reach - 1 - step) * rows
        store_k = lax.dynamic_update_slice_in_dim(store_k, piece_k, slot, 0)
        store_v = lax.dynamic_update_slice_in_dim(store_v, piece_v, slot, 0)
        return (piece_k, piece_v, store_k, store_v)

    carried = lax.fori_loop(0, reach, bring, (attn_key, attn_value, buffer_k, buffer_v))
    buffer_k = carried[2].reshape((reach + 1) * rows, KV_HEADS, HEAD_DIM)
    buffer_v = carried[3].reshape((reach + 1) * rows, KV_HEADS, HEAD_DIM)
    device_pos = lax.axis_index("seq") * lax.axis_size("head") + lax.axis_index("head")
    t_pos = device_pos * rows + jnp.arange(rows, dtype=jnp.int32)
    s_pos = (device_pos - reach) * rows + jnp.arange((reach + 1) * rows, dtype=jnp.int32)
    gap = t_pos[:, None] - s_pos[None, :]
    keep = (gap >= 0) & (gap < WINDOW) & (s_pos[None, :] >= 0)
    query_heads = attn_query.reshape(rows, KV_HEADS, group, HEAD_DIM)
    scaling = 1.0 / math.sqrt(HEAD_DIM)
    scores = (
        jnp.einsum("fcgd,lcd->cgfl", query_heads, buffer_k, preferred_element_type=jnp.float32)
        * scaling
    )
    scores = jnp.where(keep, scores, -1e30)
    top = jnp.max(scores, axis=-1, keepdims=True)
    expo = jnp.exp(scores - top)
    probs = (expo / jnp.sum(expo, axis=-1, keepdims=True)).astype(jnp.bfloat16)
    attn_out = jnp.einsum("cgfl,lcd->fcgd", probs, buffer_v, preferred_element_type=jnp.float32)
    attn_out = attn_out.reshape(rows, Q_HEADS * HEAD_DIM)
    return (attn_out + fw_fine.astype(jnp.float32)).astype(jnp.bfloat16)

MESH = pl.DeviceIdType.MESH
LANES = 128


def gray(i):
    return i + (i // 2) * (1 - 2 * (i % 2))


def fused_kernel(
    heads, width, rows,
    q_hbm, k_hbm, v_hbm, rate_ref, w_hbm, aq_hbm, ak_hbm, av_hbm, out_ref,
    qb, kb, vb, wb, aqb, akb, avb, g, r0, r1, r2, r3, nw, att, bias, fsend, frecv,
    in_sem, misc_sem, halo_s, halo_r, s0_s, s0_r, s1_s, s1_r, s2_s, s2_r, s3_s, s3_r,
    za_s, za_r, zb_s, zb_r, x_s, x_r, c_s, c_r, y_s, y_r,
):
    me = lax.axis_index("seq")
    y = lax.axis_index("head")
    n_seq, n_head = lax.axis_size("seq"), lax.axis_size("head")
    core, xx, zb0, zb1 = me % 2, (me // 2) % 2, (me // 4) % 2, me // 8
    z = me // 4
    cb = core * 2 + xx
    other_core = me + 1 - 2 * core
    other_x = me + 2 - 4 * xx
    z_near = me + 4 - 8 * zb0
    z_far = me + 8 - 16 * zb1
    pos = me * n_head + y
    last = n_seq * n_head
    extra = WINDOW - rows
    pad = akb.shape[0] - WINDOW - rows

    def cols(block, size=LANES):
        return pl.ds(pl.multiple_of(block * size, size), size)

    def remote(src, dst, ssem, rsem, seq, head=None):
        return pltpu.make_async_remote_copy(
            src_ref=src, dst_ref=dst, send_sem=ssem, recv_sem=rsem,
            device_id={"seq": seq, "head": y if head is None else head},
            device_id_type=MESH,
        )

    def loads(h):
        c = cols(h, width)
        return (
            pltpu.make_async_copy(k_hbm.at[:, c], kb.at[:, c], in_sem.at[h, 0]),
            pltpu.make_async_copy(v_hbm.at[:, c], vb.at[:, c], in_sem.at[h, 1]),
            pltpu.make_async_copy(w_hbm.at[:, h], wb.at[:, h], in_sem.at[h, 2]),
        )

    own_at = pl.ds(pad + WINDOW, rows)
    others = (
        pltpu.make_async_copy(aq_hbm, aqb, misc_sem.at[0]),
        pltpu.make_async_copy(ak_hbm, akb.at[own_at], misc_sem.at[1]),
        pltpu.make_async_copy(av_hbm, avb.at[own_at], misc_sem.at[2]),
        pltpu.make_async_copy(q_hbm, qb, misc_sem.at[3]),
    )
    for i in range(heads):
        for copy in loads(i + (i // 2) * (1 - 2 * (i % 2))):
            copy.start()
    for copy in others:
        copy.start()

    barrier = pltpu.get_barrier_semaphore()

    def greet(seq, head):
        pl.semaphore_signal(barrier, inc=1, device_id={"seq": seq, "head": head}, device_id_type=MESH)

    for seq in (other_core, other_x, z_near, z_far):
        greet(seq, y)
    greet(me, 1 - y)

    for step in (1, 2):
        for there in (pos + step, pos + last - step):
            there = there % last
            greet(there // n_head, there % n_head)
    pl.semaphore_wait(barrier, 9)

    def halo(step):
        there = pos + step
        seq, head = there // n_head, there % n_head
        if step == 1:
            src, dst = pl.ds(0, rows), pl.ds(pad + extra, rows)
        else:
            src, dst = pl.ds(rows - extra, extra), pl.ds(pad, extra)
        j = (step - 1) * 2
        return (
            remote(ak_hbm.at[src], akb.at[dst], halo_s.at[j], halo_r.at[j], seq, head),
            remote(av_hbm.at[src], avb.at[dst], halo_s.at[j + 1], halo_r.at[j + 1], seq, head),
        )

    for step in (1, 2):
        @pl.when(pos + step < last)
        def _():
            for copy in halo(step):
                copy.start()

        @pl.when(pos < step)
        def _():
            at = pl.ds(pad + extra, rows) if step == 1 else pl.ds(pad, extra)
            akb[at, :] = jnp.zeros((at.size, akb.shape[1]), akb.dtype)
            avb[at, :] = jnp.zeros((at.size, avb.shape[1]), avb.dtype)

    akb[pl.ds(0, pad), :] = jnp.zeros((pad, akb.shape[1]), akb.dtype)
    avb[pl.ds(0, pad), :] = jnp.zeros((pad, avb.shape[1]), avb.dtype)
    t_idx = lax.broadcasted_iota(jnp.int32, bias.shape, 0)
    s_idx = lax.broadcasted_iota(jnp.int32, bias.shape, 1) - (pad + WINDOW)
    gap = t_idx - s_idx
    keep = (gap >= 0) & (gap < WINDOW) & (s_idx + pos * rows >= 0)
    bias[...] = keep.astype(jnp.float32)

    def s0(h, m):
        return remote(
            g.at[h, m, :, cols(1 - core, 2 * LANES)], r0.at[h, m], s0_s.at[h, m], s0_r.at[h, m], other_core
        )

    def s1(h, m):
        return remote(
            g.at[h, m, :, cols(core * 2 + 1 - xx)], r1.at[h, m], s1_s.at[h, m], s1_r.at[h, m], other_x
        )

    def s2(h, m):
        return remote(
            g.at[h, m, :, cols(cb)], r2.at[h // 2, m], s2_s.at[h // 2, m], s2_r.at[h // 2, m], z_near
        )

    def s3(h, m):
        return remote(g.at[h, m, :, cols(cb)], r3.at[m], s3_s.at[m], s3_r.at[m], z_far)

    def add(h, m, block, piece):
        mine = g[h, m, :, cols(block)].astype(jnp.float32)
        g[h, m, :, cols(block)] = (mine + piece.astype(jnp.float32)).astype(g.dtype)

    def compute(h):
        for copy in loads(h):
            copy.wait()
        c = cols(h, width)
        keys = kb[:, c]
        head_lane = lax.broadcasted_iota(jnp.int32, rate_ref.shape, 1)
        rate = jnp.sum(jnp.where(head_lane == h, rate_ref[...], 0.0), axis=1, keepdims=True)
        scaled = (rate * vb[:, c].astype(jnp.float32)).astype(jnp.bfloat16)
        pre_gate = jnp.dot(keys, wb[0, h], preferred_element_type=jnp.float32)
        pre_up = jnp.dot(keys, wb[1, h], preferred_element_type=jnp.float32)
        sigm = jax.nn.sigmoid(pre_gate)
        hidden = (pre_gate * sigm * pre_up).astype(jnp.bfloat16)
        tn = (((0,), (0,)), ((), ()))

        def put(m, left, right):
            g[h, m] = lax.dot_general(left, right, tn, preferred_element_type=jnp.float32).astype(g.dtype)
            s0(h, m).start()

        put(2, hidden, scaled)
        back = lax.dot_general(
            scaled, wb[2, h], (((1,), (1,)), ((), ())), preferred_element_type=jnp.float32
        )
        d_up = (back * pre_gate * sigm).astype(jnp.bfloat16)
        put(1, keys, d_up)
        d_gate = (back * pre_up * sigm * (1.0 + pre_gate * (1.0 - sigm))).astype(jnp.bfloat16)
        put(0, keys, d_gate)

    def first_add(h):
        def one(j, _):
            m = 2 - j
            s0(h, m).wait_recv()
            add(h, m, core * 2 + 1 - xx, r0[h, m, :, cols(1 - xx)])
            s1(h, m).start()
            add(h, m, cb, r0[h, m, :, cols(xx)])
            return 0

        lax.fori_loop(0, 3, one, 0)

    def loop_a(i, _):
        compute(gray(i))

        @pl.when(i > 0)
        def _():
            first_add(gray(i - 1))

        return 0

    lax.fori_loop(0, heads, loop_a, 0)
    first_add(gray(heads - 1))

    group = Q_HEADS // KV_HEADS
    scaling = 1.0 / math.sqrt(HEAD_DIM)

    def attend(c):
        keys = akb[:, cols(c)]
        vals = avb[:, cols(c)]
        for j in range(group):
            qc = cols(c * group + j)
            scores = lax.dot_general(
                aqb[:, qc], keys, (((1,), (1,)), ((), ())), preferred_element_type=jnp.float32
            ) * scaling
            scores = jnp.where(bias[...] > 0.0, scores, -1e30)
            top = jnp.max(scores, axis=-1, keepdims=True)
            expo = jnp.exp(scores - top)
            probs = (expo / jnp.sum(expo, axis=-1, keepdims=True)).astype(jnp.bfloat16)
            att[:, qc] = jnp.dot(probs, vals, preferred_element_type=jnp.float32)

    def share(h, m, block):
        return nw.at[h, m, :, cols(block)]

    def far(h, m):
        return remote(share(h, m, cb), share(h, m, cb), za_s.at[m], za_r.at[m], z_far)

    def near(h, m):
        b = h // 2
        return remote(share(h, m, cb), share(h, m, cb), zb_s.at[b, m], zb_r.at[b, m], z_near)

    def near_from(h, m):
        return near(h, m)

    def side(h, m):
        return remote(share(h, m, cb), share(h, m, cb), x_s.at[h, m], x_r.at[h, m], other_x)

    def pair(h, m, x_of):
        block = core * 2 + x_of
        return remote(
            share(h, m, block), share(h, m, block), c_s.at[h, m, x_of], c_r.at[h, m, x_of], other_core
        )

    def side_from(h, m):
        block = core * 2 + 1 - xx
        return remote(share(h, m, block), share(h, m, block), x_s.at[h, m], x_r.at[h, m], other_x)

    def pair_from(h, m, x_of):
        block = (1 - core) * 2 + x_of
        return remote(
            share(h, m, block), share(h, m, block), c_s.at[h, m, x_of], c_r.at[h, m, x_of], other_core
        )

    def stage2(p):
        h, m = gray(p // 3), 2 - p % 3
        s1(h, m).wait_recv()
        add(h, m, cb, r1[h, m])

        @pl.when(h % 2 != zb0)
        def _():
            s2(h, m).start()

    def stage3(p):
        h, m = gray(p // 3), 2 - p % 3

        @pl.when(h % 2 == zb0)
        def _():
            s2(h, m).wait_recv()
            add(h, m, cb, r2[h // 2, m])

            @pl.when(h // 2 != zb1)
            def _():
                s3(h, m).start()

    def stage4(p):
        h, m = gray(p // 3), 2 - p % 3

        @pl.when(h == z)
        def _():
            s3(h, m).wait_recv()
            start = wb[m, h, :, cols(cb)].astype(jnp.float32)
            total = g[h, m, :, cols(cb)].astype(jnp.float32) + r3[m].astype(jnp.float32)
            stepped = start + total
            ratio = jnp.sqrt(jnp.mean(start * start, axis=0, keepdims=True)) * lax.rsqrt(
                jnp.mean(stepped * stepped, axis=0, keepdims=True) + 1e-06
            )
            nw[h, m, :, cols(cb)] = (stepped * ratio).astype(nw.dtype)
            side(h, m).start()
            far(h, m).start()
            near(h, m).start()
            pair(h, m, xx).start()

    pieces = heads * 3
    first_att = 4
    lag3, lag4 = 5, 10

    def loop_b(t, _):
        @pl.when(t < pieces)
        def _():
            stage2(t)

        @pl.when((t >= lag3) & (t < pieces + lag3))
        def _():
            stage3(t - lag3)

        @pl.when(t >= lag4)
        def _():
            stage4(t - lag4)

        @pl.when(t == first_att)
        def _():
            for copy in others:
                copy.wait()
            for step in (1, 2):
                @pl.when(pos >= step)
                def _():
                    for copy in halo(step):
                        copy.wait_recv()

        @pl.when((t >= first_att) & (t < first_att + KV_HEADS))
        def _():
            attend(t - first_att)

        return 0

    lax.fori_loop(0, pieces + lag4, loop_b, 0)

    def answer_send(h):
        return remote(fsend.at[h], frecv.at[h], y_s.at[h], y_r.at[h], me, 1 - y)

    def head_of(i):
        return ((zb1 + i % 2) % 2) * 2 + (zb0 + i // 2) % 2

    def mix(value, group_of, h):
        at = cols(group_of * heads + h, width)
        out_ref[:, at] = (att[:, at] + value.astype(jnp.float32)).astype(out_ref.dtype)

    def loop_c(i, _):
        h = head_of(i)

        @pl.when(i == 0)
        def _():
            def one(j, _):
                m = 2 - j
                h_far = head_of(1)
                far(h_far, m).wait_recv()
                near(h_far, m).start()
                side(h_far, m).start()
                pair(h_far, m, xx).start()
                return 0

            lax.fori_loop(0, 3, one, 0)

        @pl.when(i < 2)
        def _():
            def one(j, _):
                m = 2 - j
                h_near = head_of(i + 2)
                near_from(h_near, m).wait_recv()
                side(h_near, m).start()
                pair(h_near, m, xx).start()
                return 0

            lax.fori_loop(0, 3, one, 0)

        def crossed(j, _):
            m = 2 - j
            side_from(h, m).wait_recv()
            pair(h, m, 1 - xx).start()
            return 0

        lax.fori_loop(0, 3, crossed, 0)

        def landed(m, _):
            pair_from(h, m, 0).wait_recv()
            pair_from(h, m, 1).wait_recv()
            return 0

        lax.fori_loop(0, 3, landed, 0)
        queries = qb[:, cols(h, width)]
        q_gate = jnp.dot(queries, nw[h, 0], preferred_element_type=jnp.float32)
        q_up = jnp.dot(queries, nw[h, 1], preferred_element_type=jnp.float32)
        hid = (q_gate * jax.nn.sigmoid(q_gate) * q_up).astype(jnp.bfloat16)
        full = jnp.dot(hid, nw[h, 2], preferred_element_type=jnp.float32).astype(jnp.bfloat16)
        low, high = full[:rows], full[rows:]
        lower = jnp.zeros((rows, width), jnp.int32) + y < 1
        fsend[h] = jnp.where(lower, high.astype(jnp.float32), low.astype(jnp.float32)).astype(jnp.bfloat16)
        answer_send(h).start()
        mix(jnp.where(lower, low.astype(jnp.float32), high.astype(jnp.float32)), y, h)
        return 0

    lax.fori_loop(0, heads, loop_c, 0)

    def loop_d(i, _):
        h = head_of(i)
        answer_send(h).wait_recv()
        mix(frecv[h], 1 - y, h)
        return 0

    lax.fori_loop(0, heads, loop_d, 0)

    for step in (1, 2):
        @pl.when(pos + step < last)
        def _():
            for copy in halo(step):
                copy.wait_send()

    def sent(p, _):
        h, m = p // 3, p % 3
        s0(h, m).wait_send()
        s1(h, m).wait_send()

        @pl.when(h % 2 != zb0)
        def _():
            s2(h, m).wait_send()

        @pl.when((h % 2 == zb0) & (h // 2 != zb1))
        def _():
            s3(h, m).wait_send()

        @pl.when(h == z)
        def _():
            far(h, m).wait_send()

        @pl.when(h % 2 == zb0)
        def _():
            near(h, m).wait_send()

        side(h, m).wait_send()
        pair(h, m, 0).wait_send()
        pair(h, m, 1).wait_send()
        return 0

    lax.fori_loop(0, pieces, sent, 0)

    def sent_y(h, _):
        answer_send(h).wait_send()
        return 0

    lax.fori_loop(0, heads, sent_y, 0)


def fused(fw_query, fw_key, fw_value, learn_rate, fast_weights, attn_query, attn_key, attn_value):
    tokens, heads, width = fw_key.shape[0], fast_weights.shape[1], fast_weights.shape[2]
    rows, kv_width = attn_key.shape
    span = -(-(WINDOW + rows) // LANES) * LANES
    bf, f32 = jnp.bfloat16, jnp.float32
    anywhere = pl.BlockSpec(memory_space=pl.ANY)
    vmem = pl.BlockSpec(memory_space=pltpu.VMEM)
    dma = pltpu.SemaphoreType.DMA
    half = heads // 2
    return pl.pallas_call(
        functools.partial(fused_kernel, heads, width, rows),
        out_shape=jax.ShapeDtypeStruct(attn_query.shape, bf),
        in_specs=[anywhere, anywhere, anywhere, vmem, anywhere, anywhere, anywhere, anywhere],
        out_specs=vmem,
        scratch_shapes=[
            pltpu.VMEM(fw_query.shape, bf),
            pltpu.VMEM(fw_key.shape, bf),
            pltpu.VMEM(fw_value.shape, bf),
            pltpu.VMEM(fast_weights.shape, bf),
            pltpu.VMEM(attn_query.shape, bf),
            pltpu.VMEM((span, kv_width), bf),
            pltpu.VMEM((span, kv_width), bf),
            pltpu.VMEM((heads, 3, width, width), bf),
            pltpu.VMEM((heads, 3, width, 2 * LANES), bf),
            pltpu.VMEM((heads, 3, width, LANES), bf),
            pltpu.VMEM((half, 3, width, LANES), bf),
            pltpu.VMEM((3, width, LANES), bf),
            pltpu.VMEM((heads, 3, width, width), bf),
            pltpu.VMEM(attn_query.shape, f32),
            pltpu.VMEM((rows, span), f32),
            pltpu.VMEM((heads, rows, width), bf),
            pltpu.VMEM((heads, rows, width), bf),
            dma((heads, 3)), dma((4,)), dma((4,)), dma((4,)),
            dma((heads, 3)), dma((heads, 3)), dma((heads, 3)), dma((heads, 3)),
            dma((half, 3)), dma((half, 3)), dma((3,)), dma((3,)),
            dma((3,)), dma((3,)), dma((half, 3)), dma((half, 3)),
            dma((heads, 3)), dma((heads, 3)), dma((heads, 3, 2)), dma((heads, 3, 2)),
            dma((heads,)), dma((heads,)),
        ],
        compiler_params=pltpu.CompilerParams(
            collective_id=0, has_side_effects=True, vmem_limit_bytes=60 * 1024 * 1024
        ),
    )(fw_query, fw_key, fw_value, learn_rate, fast_weights, attn_query, attn_key, attn_value)


def takes_fused(mesh, args):
    tokens, rows = args[1].shape[0], args[5].shape[0]
    heads, width = args[4].shape[1], args[4].shape[2]
    return (
        mesh.shape["seq"] == 16
        and mesh.shape["head"] == 2
        and heads == 4
        and width == 4 * LANES
        and tokens == 2 * rows
        and rows < WINDOW < 2 * rows
        and (-(WINDOW + rows)) % LANES > 0
    )


def solution(mesh):
    placed = (
        P("seq", "head"),
        P("seq", "head"),
        P("seq", "head"),
        P("seq", "head"),
        P(None, "head", None, None),
        P(("seq", "head"), None),
        P(("seq", "head"), None),
        P(("seq", "head"), None),
    )

    def body(*args):
        return fused(*args) if takes_fused(mesh, args) else on_device(*args)

    return jax.shard_map(
        body, mesh=mesh, in_specs=placed, out_specs=P(("seq", "head"), None), check_vma=False
    )
```
